768 devices in a mesh: outer: 6 (over z_lo), dp: 128 (over x, z_hi, y, core).
Axes of the slice: x: 4, y: 8, z: 12 (z_hi: 2, z_lo: 6; z = z_hi * 6 + z_lo), core: 2. Of those that a mesh axis runs over, the one named last changes fastest.
Arguments:
- grads: float32 [6, 6, 1024, 576], P('outer', None, 'dp'), may hold values from -64 to 64
- momentum: float32 [6, 1024, 576], P(None, 'dp'), may hold values from -4 to 4
Outputs:
- momentum_new: float32 [6, 1024, 576], P(None, 'dp')
- update: float32 [6, 1024, 576], P(None, 'dp')
The draws below stay inside these ranges and needn't reach their ends.
All inputs are finite; a program needn't handle non-finite values.
Results may differ from the reference program's by a relative error of at most 0.0057.
Values may be sent and summed in bfloat16 or wider, within the bound.
A program may use at most 32 MiB of HBM per device.

```python
import math
import jax
import jax.numpy as jnp
from jax import lax

R = 1024
C = 576
ITERS = 2
PODS = 6
MATS = 6


def draw_grads(key, part):
    key_noise, key_row, key_col = jax.random.split(key, 3)
    noise = jax.random.normal(key_noise, (PODS, MATS, R, C), jnp.float32)
    row_top = math.log(10.0)
    noise = jnp.clip(noise, -4.0, 4.0)
    row_scale = jnp.exp(row_top * jax.random.uniform(key_row, (1, MATS, R, 1), jnp.float32))
    col_scale = jnp.exp(math.log(10.0) * jax.random.uniform(key_col, (1, MATS, 1, C), jnp.float32))
    trend = jnp.exp(math.log(3.0) * jnp.arange(R, dtype=jnp.float32) / (R - 1)).reshape(1, 1, R, 1)
    return noise * row_scale * col_scale * trend / 30.0


def steps_of(stream_key, extent, cuts, least, high):
    def one(axis_at, shards_of):
        heights = jax.random.uniform(jax.random.fold_in(jax.random.fold_in(stream_key, 6), axis_at), (shards_of,), jnp.float32, least / len(cuts), high / len(cuts))
        return jnp.repeat(jnp.exp(heights), extent[axis_at] // shards_of).reshape((-1,) + (1,) * (len(extent) - axis_at - 1))

    loudness = one(*cuts[0])
    for cut in cuts[1:]:
        loudness = loudness * one(*cut)
    return loudness


def centred(rng, dims, deviation, bound, pieces=(), kind=jnp.bfloat16):
    array = deviation * jax.random.normal(rng, dims, jnp.float32)
    if pieces:
        array = array * steps_of(rng, dims, pieces, -0.22, 0.18)
    return jnp.clip(array, -bound, bound).astype(kind)


def setup_inputs(seed: int = 0) -> dict:
    key_of = jax.random.split(jax.random.key(seed), 3)
    return {
        "grads": draw_grads(jax.random.fold_in(key_of[2], 71), 0),
        "momentum": centred(key_of[1], (MATS, R, C), 0.5, 4.0, ((1, 128),), jnp.float32),
    }


coef_a = 3.4445
coef_b = -4.775
coef_c = 2.0315
momentum_rate = 0.95
epsilon = 1e-06

def gram_product(matrix):
    return lax.dot_general(matrix, matrix, (((0,), (0,)), ((), ())), preferred_element_type=jnp.float32)

def newton_steps(matrix):
    for iteration in range(ITERS):
        gram_matrix = gram_product(matrix).astype(jnp.bfloat16)
        squared = jnp.dot(gram_matrix, gram_matrix, preferred_element_type=jnp.float32)
        polynomial = (coef_b * gram_matrix.astype(jnp.float32) + coef_c * squared).astype(jnp.bfloat16)
        mixed = jnp.dot(matrix, polynomial, preferred_element_type=jnp.float32)
        matrix = (coef_a * matrix.astype(jnp.float32) + mixed).astype(jnp.bfloat16)
    return matrix

def orthogonalize(steering):
    values = steering.astype(jnp.float32)
    norm_value = jnp.sqrt(jnp.sum(values * values))
    start = (values / (norm_value + epsilon)).astype(jnp.bfloat16)
    return newton_steps(start)

def reference(grads, momentum):
    summed = lax.optimization_barrier(jnp.sum(grads, axis=0))
    momentum_new = momentum_rate * momentum + summed
    steering = (summed + momentum_rate * momentum_new).astype(jnp.bfloat16)
    orthogonal = lax.map(orthogonalize, steering)
    update_scale = 0.2 * math.sqrt(max(R, C))
    return (momentum_new, update_scale * orthogonal.astype(jnp.float32))
```

```python
import functools
import math

import jax
import jax.numpy as jnp
from jax import lax
from jax.experimental import pallas as pl
from jax.experimental.pallas import tpu as pltpu
from jax.sharding import PartitionSpec as P

MESH = pl.DeviceIdType.MESH

coef_a = 3.4445
coef_b = -4.775
coef_c = 2.0315
momentum_rate = 0.95
epsilon = 1e-06

PODS = 6
NX = 4
NY = 8
CORES = 2
LANES = 128


def dot(left, right):
    return jnp.dot(left, right, preferred_element_type=jnp.float32)


def gram_product(matrix):
    return lax.dot_general(
        matrix, matrix, (((0,), (0,)), ((), ())), preferred_element_type=jnp.float32
    )


def kernel(
    scale,
    grads,
    momentum,
    momentum_out,
    update_out,
    own_grad,
    own_momentum,
    parts,
    moments,
    block,
    mirror_block,
    rows,
    finals,
    result,
    local_sem,
    part_send,
    part_recv,
    moment_send,
    moment_recv,
    mirror_send,
    mirror_recv,
    y_send,
    y_recv,
    x_send,
    x_recv,
    core_send,
    core_recv,
    final_send,
    final_recv,
):
    width = grads.shape[-1]
    wide = rows.shape[-1]
    pod = lax.axis_index("outer")
    dp = lax.axis_index("dp")
    core = lax.rem(dp, 2)
    y = lax.rem(dp // 2, NY)
    half = lax.rem(dp // (2 * NY), 2)
    x = dp // (4 * NY)

    def dp_of(x_, half_, y_, core_):
        return ((x_ * 2 + half_) * NY + y_) * 2 + core_

    def matrix_of(pod_):
        return pod_ + half * (PODS - 1 - 2 * pod_)

    mine = matrix_of(pod)
    pods = [lax.rem(pod + d, PODS) for d in range(1, PODS)]
    mirror = (PODS - 1 - pod, dp_of(x, 1 - half, y, core))
    along_y = [(pod, dp_of(x, half, lax.rem(y + k, NY), core)) for k in range(1, NY)]
    along_x = [(pod, dp_of(lax.rem(x + k, NX), half, y, core)) for k in range(1, NX)]
    sibling = (pod, dp_of(x, half, y, 1 - core))

    load_grad = pltpu.make_async_copy(grads.at[0, mine], own_grad, local_sem.at[0])
    load_momentum = pltpu.make_async_copy(momentum.at[mine], own_momentum, local_sem.at[1])
    load_grad.start()
    load_momentum.start()

    barrier = pltpu.get_barrier_semaphore()
    peers = [(p, dp) for p in pods] + [mirror] + along_y + along_x + [sibling]
    for peer in peers:
        pl.semaphore_signal(barrier, inc=1, device_id=peer, device_id_type=MESH)
    pl.semaphore_wait(barrier, len(peers))

    def remote(source, target, send_sem, recv_sem, device):
        return pltpu.make_async_remote_copy(
            src_ref=source,
            dst_ref=target,
            send_sem=send_sem,
            recv_sem=recv_sem,
            device_id=device,
            device_id_type=MESH,
        )

    sent = []
    for d, p in enumerate(pods):
        copy = remote(
            grads.at[0, matrix_of(p)], parts.at[d], part_send.at[d], part_recv.at[d], (p, dp)
        )
        copy.start()
        sent.append(copy)
    block[...] = jnp.zeros_like(block)
    load_grad.wait()
    load_momentum.wait()
    summed = own_grad[...]
    for d, copy in enumerate(sent):
        copy.wait_recv()
        summed = summed + parts[d]
    momentum_new = momentum_rate * own_momentum[...] + summed
    steering = summed + momentum_rate * momentum_new
    block[:, :width] = steering.astype(jnp.bfloat16)

    to_mirror = remote(block, mirror_block, mirror_send, mirror_recv, mirror)
    to_mirror.start()
    sent.append(to_mirror)
    moments[mine] = momentum_new
    to_mirror.wait_recv()
    pair = jnp.concatenate(
        [block[...].astype(jnp.float32), mirror_block[...].astype(jnp.float32)], axis=0
    )
    rows[core, x, y] = pair.astype(jnp.bfloat16)

    to_y = []
    for k, peer in enumerate(along_y):
        here = rows.at[core, x, y]
        copy = remote(here, here, y_send.at[k], y_recv.at[k], peer)
        copy.start()
        to_y.append(copy)
    to_pods = []
    for d, p in enumerate(pods):
        here = moments.at[mine]
        copy = remote(here, here, moment_send.at[d], moment_recv.at[d], (p, dp))
        copy.start()
        to_pods.append(copy)
    for copy in to_y:
        copy.wait_recv()

    to_x = []
    here = rows.at[core, x]
    for k, peer in enumerate(along_x):
        copy = remote(here, here, x_send.at[k], x_recv.at[k], peer)
        copy.start()
        to_x.append(copy)
    to_core = [remote(here, here, core_send.at[0], core_recv.at[0], sibling)]
    to_core[0].start()
    for k in range(1, NX):
        to_x[k - 1].wait_recv()
        there = rows.at[core, lax.rem(x - k + NX, NX)]
        copy = remote(there, there, core_send.at[k], core_recv.at[k], sibling)
        copy.start()
        to_core.append(copy)
    for copy in to_core:
        copy.wait_recv()

    raw = gram_product(rows[...].reshape(-1, wide))
    down = lax.broadcasted_iota(jnp.int32, (wide, wide), 0)
    across = lax.broadcasted_iota(jnp.int32, (wide, wide), 1)
    trace = jnp.sum(jnp.where(down == across, raw, 0.0), keepdims=True)
    inverse = 1.0 / (jnp.sqrt(trace) + epsilon)
    gram = (raw * (inverse * inverse)).astype(jnp.bfloat16)
    start = (pair * inverse).astype(jnp.bfloat16)
    polynomial = (coef_b * gram.astype(jnp.float32) + coef_c * dot(gram, gram)).astype(
        jnp.bfloat16
    )
    first = (coef_a * start.astype(jnp.float32) + dot(start, polynomial)).astype(jnp.bfloat16)
    half_way = (coef_a * gram.astype(jnp.float32) + dot(gram, polynomial)).astype(jnp.bfloat16)
    gram = (coef_a * half_way.astype(jnp.float32) + dot(polynomial, half_way)).astype(
        jnp.bfloat16
    )
    polynomial = (coef_b * gram.astype(jnp.float32) + coef_c * dot(gram, gram)).astype(
        jnp.bfloat16
    )
    second = coef_a * first.astype(jnp.float32) + dot(first, polynomial)
    finals[mine] = second[: block.shape[0]].astype(jnp.bfloat16)

    to_finals = []
    here = finals.at[mine]
    for d, p in enumerate(pods):
        copy = remote(here, here, final_send.at[d], final_recv.at[d], (p, dp))
        copy.start()
        to_finals.append(copy)
    for copy in to_pods:
        copy.wait_recv()
    store_moments = pltpu.make_async_copy(moments, momentum_out, local_sem.at[0])
    store_moments.start()
    for copy in to_finals:
        copy.wait_recv()
    result[...] = scale * finals[:, :, :width].astype(jnp.float32)
    store_update = pltpu.make_async_copy(result, update_out, local_sem.at[1])
    store_update.start()
    for copy in sent + to_y + to_pods + to_x + to_core + to_finals:
        copy.wait_send()
    store_moments.wait()
    store_update.wait()


def per_device(grads, momentum):
    _, count, depth, width = grads.shape
    wide = -(-width // LANES) * LANES
    height = depth * NX * 2 * NY * CORES
    scale = 0.2 * math.sqrt(max(height, width))
    half, single = jnp.bfloat16, jnp.float32
    dma = pltpu.SemaphoreType.DMA
    return pl.pallas_call(
        functools.partial(kernel, scale),
        out_shape=[jax.ShapeDtypeStruct(momentum.shape, single)] * 2,
        in_specs=[pl.BlockSpec(memory_space=pl.ANY)] * 2,
        out_specs=[pl.BlockSpec(memory_space=pl.ANY)] * 2,
        scratch_shapes=[
            pltpu.VMEM((depth, width), single),
            pltpu.VMEM((depth, width), single),
            pltpu.VMEM((PODS - 1, depth, width), single),
            pltpu.VMEM((count, depth, width), single),
            pltpu.VMEM((depth, wide), half),
            pltpu.VMEM((depth, wide), half),
            pltpu.VMEM((CORES, NX, NY, 2 * depth, wide), half),
            pltpu.VMEM((count, depth, wide), half),
            pltpu.VMEM((count, depth, width), single),
            dma((2,)),
            dma((PODS - 1,)),
            dma((PODS - 1,)),
            dma((PODS - 1,)),
            dma((PODS - 1,)),
            dma,
            dma,
            dma((NY - 1,)),
            dma((NY - 1,)),
            dma((NX - 1,)),
            dma((NX - 1,)),
            dma((NX,)),
            dma((NX,)),
            dma((PODS - 1,)),
            dma((PODS - 1,)),
        ],
        compiler_params=pltpu.CompilerParams(collective_id=0, has_side_effects=True),
    )(grads, momentum)


def solution(mesh):
    in_specs = (P("outer", None, "dp", None), P(None, "dp", None))
    out_specs = (P(None, "dp", None), P(None, "dp", None))
    return jax.shard_map(
        per_device, mesh=mesh, in_specs=in_specs, out_specs=out_specs, check_vma=False
    )
```

```python
import functools
import math

import jax
import jax.numpy as jnp
from jax import lax
from jax.experimental import pallas as pl
from jax.experimental.pallas import tpu as pltpu
from jax.sharding import PartitionSpec as P

MESH = pl.DeviceIdType.MESH

coef_a = 3.4445
coef_b = -4.775
coef_c = 2.0315
momentum_rate = 0.95
epsilon = 1e-06

PODS = 6
NZ = 12
NX = 4
NY = 8
CORES = 2
LANES = 128
ALONG_Y = (1, 7, 2, 6, 3, 5, 4)
ALONG_X = (1, 3, 2)
GROUPS = ((0, 1), (1, 3), (3, 5), (5, 8))
FAR_MATRICES = (3, 2, 4, 1, 5, 0)
FAR_CHIPS = (6, 5, 7, 4, 8, 3, 9, 2, 10, 1, 11, 0)


def dot(left, right):
    return jnp.dot(left, right, preferred_element_type=jnp.float32)


def gram_product(matrix):
    return lax.dot_general(
        matrix, matrix, (((0,), (0,)), ((), ())), preferred_element_type=jnp.float32
    )


def kernel(
    scale,
    grads,
    momentum,
    momentum_out,
    update_out,
    my_grads,
    my_momentum,
    terms,
    parts,
    sums,
    totals,
    rows,
    raw,
    pieces,
    finals,
    result,
    local_sem,
    term_send,
    term_recv,
    y_send,
    y_recv,
    x_send,
    x_recv,
    total_send,
    total_recv,
    final_send,
    final_recv,
):
    width = grads.shape[-1]
    wide = rows.shape[-1]
    pod = lax.axis_index("outer")
    dp = lax.axis_index("dp")
    core = lax.rem(dp, 2)
    y = lax.rem(dp // 2, NY)
    half = lax.rem(dp // (2 * NY), 2)
    x = dp // (4 * NY)
    z = half * PODS + pod
    near = z // 2
    holder = jnp.logical_and(core == 1, lax.rem(z, 2) == 0)

    def device(x_, y_, z_, core_):
        return (lax.rem(z_, PODS), ((x_ * 2 + z_ // PODS) * NY + y_) * 2 + core_)

    def remote(source, target, send_sem, recv_sem, peer):
        return pltpu.make_async_remote_copy(
            src_ref=source,
            dst_ref=target,
            send_sem=send_sem,
            recv_sem=recv_sem,
            device_id=peer,
            device_id_type=MESH,
        )

    load_grads = pltpu.make_async_copy(grads.at[0], my_grads, local_sem.at[0])
    load_momentum = pltpu.make_async_copy(momentum, my_momentum, local_sem.at[1])
    load_grads.start()
    load_momentum.start()

    along_y = [device(x, lax.rem(y + k, NY), z, 1) for k in ALONG_Y]
    along_x = [device(lax.rem(x + k, NX), y, z, 1) for k in ALONG_X]
    barrier = pltpu.get_barrier_semaphore()

    def greet(peer):
        pl.semaphore_signal(barrier, inc=1, device_id=peer, device_id_type=MESH)

    @pl.when(holder)
    def _():
        for d in FAR_CHIPS:
            for c in range(CORES):
                if (d, c) != (0, 1):
                    greet(device(x, y, lax.rem(z + d, NZ), c))
        for peer in along_y + along_x:
            greet(peer)

    @pl.when(jnp.logical_not(holder))
    def _():
        for s in FAR_MATRICES:
            greet(device(x, y, 2 * lax.rem(near + s, PODS), 1))

    load_grads.wait()
    load_momentum.wait()
    terms[...] = (1 + momentum_rate) * my_grads[...] + (
        momentum_rate * momentum_rate / PODS
    ) * my_momentum[...]

    @pl.when(holder)
    def _():
        pl.semaphore_wait(barrier, NZ * CORES - 1 + len(along_y) + len(along_x))

    @pl.when(jnp.logical_not(holder))
    def _():
        pl.semaphore_wait(barrier, PODS)

    def term_copy(s):
        j = lax.rem(near + s, PODS)
        return remote(
            terms.at[j],
            parts.at[z, core],
            term_send.at[s],
            term_recv.at[z, core],
            device(x, y, 2 * j, 1),
        )

    for s in FAR_MATRICES:
        if s:
            term_copy(s).start()

    @pl.when(jnp.logical_not(holder))
    def _():
        term_copy(0).start()

    @pl.when(holder)
    def _():
        parts[z, 1] = terms[near]
        rows[0, 0] = jnp.zeros_like(rows[0, 0])
        for z_ in range(NZ):
            for c in range(CORES):
                arrived = remote(
                    terms.at[0],
                    parts.at[z_, c],
                    term_send.at[0],
                    term_recv.at[z_, c],
                    device(x, y, z, 0),
                )
                if c == 1 and z_ % 2 == 0:
                    pl.when(z_ != z)(arrived.wait_recv)
                else:
                    arrived.wait_recv()
        for h in range(2):
            total = parts[h * PODS]
            for k in range(1, PODS):
                total = total + parts[h * PODS + k]
            sums[pl.ds(h * CORES, CORES)] = total
        steering = sums[...].reshape(-1, width).astype(jnp.bfloat16)
        rows[0, 0, :, :width] = steering

        to_y = []
        for i, peer in enumerate(along_y):
            copy = remote(rows.at[0, 0], rows.at[0, i + 1], y_send.at[i], y_recv.at[i], peer)
            copy.start()
            to_y.append(copy)
        to_x = [[] for _ in along_x]
        for g, (low, high) in enumerate(GROUPS):
            for i in range(max(low, 1), high):
                to_y[i - 1].wait_recv()
            for i, peer in enumerate(along_x):
                copy = remote(
                    rows.at[0, pl.ds(low, high - low)],
                    rows.at[i + 1, pl.ds(low, high - low)],
                    x_send.at[i, g],
                    x_recv.at[i, g],
                    peer,
                )
                copy.start()
                to_x[i].append(copy)

        def total_copy(d, c):
            z_ = lax.rem(z + d, NZ)
            return remote(
                sums.at[(z_ // PODS) * CORES + c],
                totals.at[near],
                total_send.at[d, c],
                total_recv.at[near],
                device(x, y, z_, c),
            )

        for d in FAR_CHIPS:
            for c in range(CORES):
                if (d, c) != (0, 1):
                    total_copy(d, c).start()
        totals[near] = sums[half * CORES + 1]

        raw[...] = gram_product(rows[0].reshape(-1, wide))
        for i in range(len(along_x)):
            for copy in to_x[i]:
                copy.wait_recv()
            raw[...] += gram_product(rows[i + 1].reshape(-1, wide))

        down = lax.broadcasted_iota(jnp.int32, (wide, wide), 0)
        across = lax.broadcasted_iota(jnp.int32, (wide, wide), 1)
        trace = jnp.sum(jnp.where(down == across, raw[...], 0.0), keepdims=True)
        inverse = 1.0 / (jnp.sqrt(trace) + epsilon)
        gram = (raw[...] * (inverse * inverse)).astype(jnp.bfloat16)
        start = (rows[0, 0].astype(jnp.float32) * inverse).astype(jnp.bfloat16)
        polynomial = (
            coef_b * gram.astype(jnp.float32) + coef_c * dot(gram, gram)
        ).astype(jnp.bfloat16)
        first = (coef_a * start.astype(jnp.float32) + dot(start, polynomial)).astype(
            jnp.bfloat16
        )
        half_way = (coef_a * gram.astype(jnp.float32) + dot(gram, polynomial)).astype(
            jnp.bfloat16
        )
        gram = (coef_a * half_way.astype(jnp.float32) + dot(polynomial, half_way)).astype(
            jnp.bfloat16
        )
        polynomial = (
            coef_b * gram.astype(jnp.float32) + coef_c * dot(gram, gram)
        ).astype(jnp.bfloat16)
        second = coef_a * first.astype(jnp.float32) + dot(first, polynomial)
        depth = pieces.shape[1]
        for q in range(2 * CORES):
            pieces[q] = second[q * depth : (q + 1) * depth].astype(jnp.bfloat16)

        def final_copy(d, c):
            z_ = lax.rem(z + d, NZ)
            return remote(
                pieces.at[(z_ // PODS) * CORES + c],
                finals.at[near],
                final_send.at[d, c],
                final_recv.at[near],
                device(x, y, z_, c),
            )

        for d in FAR_CHIPS:
            for c in range(CORES):
                if (d, c) != (0, 1):
                    final_copy(d, c).start()
        finals[near] = pieces[half * CORES + 1]
        for copy in to_y + sum(to_x, []):
            copy.wait_send()
        for d in FAR_CHIPS:
            for c in range(CORES):
                if (d, c) != (0, 1):
                    total_copy(d, c).wait_send()
                    final_copy(d, c).wait_send()

    def await_matrices(buffer, sem):
        for j in range(PODS):
            arrived = remote(
                buffer.at[j], buffer.at[j], term_send.at[0], sem.at[j], device(x, y, z, 1 - core)
            )
            pl.when(jnp.logical_not(jnp.logical_and(holder, near == j)))(arrived.wait_recv)

    await_matrices(totals, total_recv)
    my_momentum[...] = (1 / (1 + momentum_rate)) * totals[...] + (
        momentum_rate - momentum_rate * momentum_rate / (1 + momentum_rate)
    ) * my_momentum[...]
    store_momentum = pltpu.make_async_copy(my_momentum, momentum_out, local_sem.at[0])
    store_momentum.start()
    await_matrices(finals, final_recv)
    result[...] = scale * finals[:, :, :width].astype(jnp.float32)
    store_update = pltpu.make_async_copy(result, update_out, local_sem.at[1])
    store_update.start()
    for s in FAR_MATRICES:
        if s:
            term_copy(s).wait_send()

    @pl.when(jnp.logical_not(holder))
    def _():
        term_copy(0).wait_send()

    store_momentum.wait()
    store_update.wait()


def per_device(grads, momentum):
    _, count, depth, width = grads.shape
    wide = -(-width // LANES) * LANES
    height = depth * NX * 2 * NY * CORES
    scale = 0.2 * math.sqrt(max(height, width))
    half, single = jnp.bfloat16, jnp.float32
    dma = pltpu.SemaphoreType.DMA
    return pl.pallas_call(
        functools.partial(kernel, scale),
        out_shape=[jax.ShapeDtypeStruct(momentum.shape, single)] * 2,
        in_specs=[pl.BlockSpec(memory_space=pl.ANY)] * 2,
        out_specs=[pl.BlockSpec(memory_space=pl.ANY)] * 2,
        scratch_shapes=[
            pltpu.VMEM((count, depth, width), single),
            pltpu.VMEM((count, depth, width), single),
            pltpu.VMEM((count, depth, width), single),
            pltpu.VMEM((NZ, CORES, depth, width), single),
            pltpu.VMEM((2 * CORES, depth, width), single),
            pltpu.VMEM((count, depth, width), single),
            pltpu.VMEM((NX, NY, 2 * CORES * depth, wide), half),
            pltpu.VMEM((wide, wide), single),
            pltpu.VMEM((2 * CORES, depth, wide), half),
            pltpu.VMEM((count, depth, wide), half),
            pltpu.VMEM((count, depth, width), single),
            dma((2,)),
            dma((PODS,)),
            dma((NZ, CORES)),
            dma((NY - 1,)),
            dma((NY - 1,)),
            dma((NX - 1, len(GROUPS))),
            dma((NX - 1, len(GROUPS))),
            dma((NZ, CORES)),
            dma((PODS,)),
            dma((NZ, CORES)),
            dma((PODS,)),
        ],
        compiler_params=pltpu.CompilerParams(collective_id=0, has_side_effects=True),
    )(grads, momentum)


def solution(mesh):
    in_specs = (P("outer", None, "dp", None), P(None, "dp", None))
    out_specs = (P(None, "dp", None), P(None, "dp", None))
    return jax.shard_map(
        per_device, mesh=mesh, in_specs=in_specs, out_specs=out_specs, check_vma=False
    )
```

```python
import functools
import math

import jax
import jax.numpy as jnp
from jax import lax
from jax.experimental import pallas as pl
from jax.experimental.pallas import tpu as pltpu
from jax.sharding import PartitionSpec as P

MESH = pl.DeviceIdType.MESH

coef_a = 3.4445
coef_b = -4.775
coef_c = 2.0315
momentum_rate = 0.95
epsilon = 1e-06

PODS = 6
NZ = 12
NX = 4
NY = 8
CORES = 2
LANES = 128
HOLDERS = (0, 2, 4, 6, 8, 10)
VMEM_LIMIT = 24 << 20
ALONG_Y = (4, 3, 5, 2, 6, 1, 7)
ALONG_X = (1, 3, 2)
GROUPS = ((0, 4), (4, 6), (6, 8))
FAR_MATRICES = (3, 2, 4, 1, 5, 0)


def hold(j):
    if isinstance(j, int):
        return HOLDERS[j]
    return sum(jnp.where(j == k, HOLDERS[k], 0) for k in range(PODS))


def slot(y):
    return jnp.where(y < NY // 2, y, 3 * NY // 2 - 1 - y)


def dot(left, right):
    return jnp.dot(left, right, preferred_element_type=jnp.float32)


def gram_product(matrix):
    return lax.dot_general(
        matrix, matrix, (((0,), (0,)), ((), ())), preferred_element_type=jnp.float32
    )


def kernel(
    grads,
    momentum,
    totals,
    finals,
    my_grads,
    my_momentum,
    terms,
    parts,
    sums,
    rows,
    raw,
    pieces,
    local_sem,
    term_send,
    term_recv,
    y_send,
    y_recv,
    x_send,
    x_recv,
    total_send,
    total_recv,
    final_send,
    final_recv,
):
    width = grads.shape[-1]
    wide = rows.shape[-1]
    pod = lax.axis_index("outer")
    dp = lax.axis_index("dp")
    core = lax.rem(dp, 2)
    y = lax.rem(dp // 2, NY)
    half = lax.rem(dp // (2 * NY), 2)
    x = dp // (4 * NY)
    z = half * PODS + pod
    near = sum(jnp.where(z == HOLDERS[k], k, 0) for k in range(PODS))
    holder = jnp.logical_and(core == 1, hold(near) == z)
    near = jnp.where(hold(near) == z, near, z // 2)
    place = slot(y)

    def device(x_, y_, z_, core_):
        return (lax.rem(z_, PODS), ((x_ * 2 + z_ // PODS) * NY + y_) * 2 + core_)

    def remote(source, target, send_sem, recv_sem, peer):
        return pltpu.make_async_remote_copy(
            src_ref=source,
            dst_ref=target,
            send_sem=send_sem,
            recv_sem=recv_sem,
            device_id=peer,
            device_id_type=MESH,
        )

    def for_line(act):
        for z_ in range(NZ):
            for c in range(CORES):
                if c == 1 and z_ in [hold(j) for j in range(PODS)]:
                    pl.when(z_ != z)(functools.partial(act, z_, c))
                else:
                    act(z_, c)

    load_grads = pltpu.make_async_copy(grads.at[0], my_grads, local_sem.at[0])
    load_momentum = pltpu.make_async_copy(momentum, my_momentum, local_sem.at[1])
    load_grads.start()
    load_momentum.start()

    along_y = [device(x, lax.rem(y + k, NY), z, 1) for k in ALONG_Y]
    along_x = [device(lax.rem(x + k, NX), y, z, 1) for k in ALONG_X]
    barrier = pltpu.get_barrier_semaphore()

    def greet(peer):
        pl.semaphore_signal(barrier, inc=1, device_id=peer, device_id_type=MESH)

    @pl.when(holder)
    def _():
        for d in range(NZ):
            for c in range(CORES):
                if (d, c) != (0, 1):
                    greet(device(x, y, lax.rem(z + d, NZ), c))
        for peer in along_y + along_x:
            greet(peer)

    @pl.when(jnp.logical_not(holder))
    def _():
        for s in FAR_MATRICES:
            greet(device(x, y, hold(lax.rem(near + s, PODS)), 1))

    load_grads.wait()
    load_momentum.wait()
    terms[...] = (1 + momentum_rate) * my_grads[...] + (
        momentum_rate * momentum_rate / PODS
    ) * my_momentum[...]

    @pl.when(holder)
    def _():
        pl.semaphore_wait(barrier, NZ * CORES - 1 + len(along_y) + len(along_x))

    @pl.when(jnp.logical_not(holder))
    def _():
        pl.semaphore_wait(barrier, PODS)

    def term_copy(s):
        j = lax.rem(near + s, PODS)
        return remote(
            terms.at[j],
            parts.at[z, core],
            term_send.at[s],
            term_recv.at[z, core],
            device(x, y, hold(j), 1),
        )

    for s in FAR_MATRICES:
        if s:
            term_copy(s).start()

    @pl.when(jnp.logical_not(holder))
    def _():
        term_copy(0).start()

    @pl.when(holder)
    def _():
        parts[z, 1] = terms[near]
        rows[0, place] = jnp.zeros_like(rows[0, 0])
        for z_ in range(NZ):
            for c in range(CORES):
                arrived = remote(
                    terms.at[0],
                    parts.at[z_, c],
                    term_send.at[0],
                    term_recv.at[z_, c],
                    device(x, y, z, 0),
                )
                if c == 1 and z_ in [hold(j) for j in range(PODS)]:
                    pl.when(z_ != z)(arrived.wait_recv)
                else:
                    arrived.wait_recv()
        for h in range(2):
            total = parts[h * PODS]
            for k in range(1, PODS):
                total = total + parts[h * PODS + k]
            sums[pl.ds(h * CORES, CORES)] = total
        steering = sums[...].reshape(-1, width).astype(jnp.bfloat16)
        rows[0, place, :, :width] = steering

        to_y = []
        for i, peer in enumerate(along_y):
            mine = rows.at[0, place]
            copy = remote(mine, mine, y_send.at[i], y_recv.at[place], peer)
            copy.start()
            to_y.append(copy)
        to_x = [[] for _ in along_x]
        for g, (low, high) in enumerate(GROUPS):
            for i in range(low, high):
                other = rows.at[0, i]
                arrived = remote(other, other, y_send.at[0], y_recv.at[i], along_y[0])
                pl.when(i != place)(arrived.wait_recv)
            for i, peer in enumerate(along_x):
                copy = remote(
                    rows.at[0, pl.ds(low, high - low)],
                    rows.at[i + 1, pl.ds(low, high - low)],
                    x_send.at[i, g],
                    x_recv.at[i, g],
                    peer,
                )
                copy.start()
                to_x[i].append(copy)

        def total_copy(z_, c):
            return remote(
                sums.at[(z_ // PODS) * CORES + c],
                totals.at[near],
                total_send.at[z_, c],
                total_recv.at[near],
                device(x, y, z_, c),
            )

        for_line(lambda z_, c: total_copy(z_, c).start())
        totals[near] = sums[half * CORES + 1]

        raw[...] = gram_product(rows[0].reshape(-1, wide))
        for i in range(len(along_x)):
            for copy in to_x[i]:
                copy.wait_recv()
            raw[...] += gram_product(rows[i + 1].reshape(-1, wide))

        down = lax.broadcasted_iota(jnp.int32, (LANES, LANES), 0)
        across = lax.broadcasted_iota(jnp.int32, (LANES, LANES), 1)
        diagonal = raw[:LANES, :LANES]
        for i in range(LANES, wide, LANES):
            diagonal = diagonal + raw[i : i + LANES, i : i + LANES]
        trace = jnp.sum(jnp.where(down == across, diagonal, 0.0), keepdims=True)
        inverse = 1.0 / (jnp.sqrt(trace) + epsilon)
        gram = (raw[...] * (inverse * inverse)).astype(jnp.bfloat16)
        start = (rows[0, place].astype(jnp.float32) * inverse).astype(jnp.bfloat16)
        polynomial = (
            coef_b * gram.astype(jnp.float32) + coef_c * dot(gram, gram)
        ).astype(jnp.bfloat16)

        def step(value):
            return coef_a * value + dot(value.astype(jnp.bfloat16), polynomial)

        def next_gram(value):
            return step(dot(step(value).astype(jnp.bfloat16), gram))

        first = step(start.astype(jnp.float32)).astype(jnp.bfloat16).astype(jnp.float32)
        once = next_gram(first)
        second = coef_a * first + coef_b * once + coef_c * next_gram(once)
        depth = pieces.shape[1]
        for q in range(2 * CORES):
            pieces[q] = second[q * depth : (q + 1) * depth].astype(jnp.bfloat16)

        def final_copy(z_, c):
            return remote(
                pieces.at[(z_ // PODS) * CORES + c],
                finals.at[near],
                final_send.at[z_, c],
                final_recv.at[near],
                device(x, y, z_, c),
            )

        for_line(lambda z_, c: final_copy(z_, c).start())
        finals[near] = pieces[half * CORES + 1]
        for copy in to_y + sum(to_x, []):
            copy.wait_send()
        for_line(lambda z_, c: total_copy(z_, c).wait_send())
        for_line(lambda z_, c: final_copy(z_, c).wait_send())

    def await_matrices(buffer, sem):
        for j in range(PODS):
            arrived = remote(
                buffer.at[j], buffer.at[j], term_send.at[0], sem.at[j], device(x, y, z, 1 - core)
            )
            pl.when(jnp.logical_not(jnp.logical_and(holder, near == j)))(arrived.wait_recv)

    await_matrices(totals, total_recv)
    await_matrices(finals, final_recv)
    for s in FAR_MATRICES:
        if s:
            term_copy(s).wait_send()

    @pl.when(jnp.logical_not(holder))
    def _():
        term_copy(0).wait_send()


def per_device(grads, momentum):
    _, count, depth, width = grads.shape
    wide = -(-width // LANES) * LANES
    height = depth * NX * 2 * NY * CORES
    scale = 0.2 * math.sqrt(max(height, width))
    half, single = jnp.bfloat16, jnp.float32
    dma = pltpu.SemaphoreType.DMA
    totals, finals = pl.pallas_call(
        kernel,
        out_shape=[
            jax.ShapeDtypeStruct(momentum.shape, single),
            jax.ShapeDtypeStruct((count, depth, wide), half),
        ],
        in_specs=[pl.BlockSpec(memory_space=pltpu.HBM)] * 2,
        out_specs=[pl.BlockSpec(memory_space=pltpu.VMEM)] * 2,
        scratch_shapes=[
            pltpu.VMEM((count, depth, width), single),
            pltpu.VMEM((count, depth, width), single),
            pltpu.VMEM((count, depth, width), single),
            pltpu.VMEM((NZ, CORES, depth, width), single),
            pltpu.VMEM((2 * CORES, depth, width), single),
            pltpu.VMEM((NX, NY, 2 * CORES * depth, wide), half),
            pltpu.VMEM((wide, wide), single),
            pltpu.VMEM((2 * CORES, depth, wide), half),
            dma((2,)),
            dma((PODS,)),
            dma((NZ, CORES)),
            dma((NY - 1,)),
            dma((NY,)),
            dma((NX - 1, len(GROUPS))),
            dma((NX - 1, len(GROUPS))),
            dma((NZ, CORES)),
            dma((PODS,)),
            dma((NZ, CORES)),
            dma((PODS,)),
        ],
        compiler_params=pltpu.CompilerParams(
            collective_id=0, has_side_effects=True, vmem_limit_bytes=VMEM_LIMIT
        ),
    )(
        pltpu.with_memory_space_constraint(grads, pltpu.HBM),
        pltpu.with_memory_space_constraint(momentum, pltpu.HBM),
    )
    momentum_new = (1 / (1 + momentum_rate)) * totals + (
        momentum_rate - momentum_rate * momentum_rate / (1 + momentum_rate)
    ) * momentum
    return momentum_new, scale * finals[:, :, :width].astype(single)


def solution(mesh):
    in_specs = (P("outer", None, "dp", None), P(None, "dp", None))
    out_specs = (P(None, "dp", None), P(None, "dp", None))
    return jax.shard_map(
        per_device, mesh=mesh, in_specs=in_specs, out_specs=out_specs, check_vma=False
    )
```

```python
import functools
import math

import jax
import jax.numpy as jnp
from jax import lax
from jax.experimental import pallas as pl
from jax.experimental.pallas import tpu as pltpu
from jax.sharding import PartitionSpec as P

MESH = pl.DeviceIdType.MESH

coef_a = 3.4445
coef_b = -4.775
coef_c = 2.0315
momentum_rate = 0.95
epsilon = 1e-06

PODS = 6
NZ = 12
NX = 4
NY = 8
CORES = 2
LANES = 128
HOLDERS = (0, 2, 3, 5, 8, 10)
VMEM_LIMIT = 24 << 20
ALONG_Y = (4, 3, 5, 2, 6, 1, 7)
ALONG_X = (1, 3, 2)
HANDED = {0: 0, 1: 1, 2: 0, 3: 1, 4: 0, 5: 1, 6: 0}
LAG = 4
FAR_MATRICES = (3, 2, 4, 1, 5, 0)


def hold(j):
    if isinstance(j, int):
        return HOLDERS[j]
    return sum(jnp.where(j == k, HOLDERS[k], 0) for k in range(PODS))


def slot(y):
    return jnp.where(y < NY // 2, y, 3 * NY // 2 - 1 - y)


def dot(left, right):
    return jnp.dot(left, right, preferred_element_type=jnp.float32)


def gram_product(matrix):
    return lax.dot_general(
        matrix, matrix, (((0,), (0,)), ((), ())), preferred_element_type=jnp.float32
    )


def kernel(
    grads,
    momentum,
    totals,
    finals,
    my_grads,
    my_momentum,
    terms,
    parts,
    sums,
    rows,
    raw,
    pieces,
    local_sem,
    term_send,
    term_recv,
    y_send,
    y_recv,
    x_send,
    x_recv,
    total_send,
    total_recv,
    final_send,
    final_recv,
):
    width = grads.shape[-1]
    wide = rows.shape[-1]
    pod = lax.axis_index("outer")
    dp = lax.axis_index("dp")
    core = lax.rem(dp, 2)
    y = lax.rem(dp // 2, NY)
    half = lax.rem(dp // (2 * NY), 2)
    x = dp // (4 * NY)
    z = half * PODS + pod
    near = sum(jnp.where(z == HOLDERS[k], k, 0) for k in range(PODS))
    holder = jnp.logical_and(core == 1, hold(near) == z)
    near = jnp.where(hold(near) == z, near, z // 2)
    place = slot(y)

    def device(x_, y_, z_, core_):
        return (lax.rem(z_, PODS), ((x_ * 2 + z_ // PODS) * NY + y_) * 2 + core_)

    def remote(source, target, send_sem, recv_sem, peer):
        return pltpu.make_async_remote_copy(
            src_ref=source,
            dst_ref=target,
            send_sem=send_sem,
            recv_sem=recv_sem,
            device_id=peer,
            device_id_type=MESH,
        )

    def for_line(act):
        for z_ in range(NZ):
            for c in range(CORES):
                if c == 1 and z_ in [hold(j) for j in range(PODS)]:
                    pl.when(z_ != z)(functools.partial(act, z_, c))
                else:
                    act(z_, c)

    load_grads = pltpu.make_async_copy(grads.at[0], my_grads, local_sem.at[0])
    load_momentum = pltpu.make_async_copy(momentum, my_momentum, local_sem.at[1])
    load_grads.start()
    load_momentum.start()

    along_y = [device(x, lax.rem(y + k, NY), z, 1) for k in ALONG_Y]
    along_x = [device(lax.rem(x + k, NX), y, z, 1) for k in ALONG_X]
    barrier = pltpu.get_barrier_semaphore()

    def greet(peer):
        pl.semaphore_signal(barrier, inc=1, device_id=peer, device_id_type=MESH)

    @pl.when(holder)
    def _():
        for d in range(NZ):
            for c in range(CORES):
                if (d, c) != (0, 1):
                    greet(device(x, y, lax.rem(z + d, NZ), c))
        for peer in along_y + along_x:
            greet(peer)

    @pl.when(jnp.logical_not(holder))
    def _():
        for s in FAR_MATRICES:
            greet(device(x, y, hold(lax.rem(near + s, PODS)), 1))

    load_grads.wait()
    load_momentum.wait()
    terms[...] = (1 + momentum_rate) * my_grads[...] + (
        momentum_rate * momentum_rate / PODS
    ) * my_momentum[...]

    @pl.when(holder)
    def _():
        pl.semaphore_wait(barrier, NZ * CORES - 1 + len(along_y) + len(along_x))

    @pl.when(jnp.logical_not(holder))
    def _():
        pl.semaphore_wait(barrier, PODS)

    def term_copy(s):
        j = lax.rem(near + s, PODS)
        return remote(
            terms.at[j],
            parts.at[z, core],
            term_send.at[s],
            term_recv.at[z, core],
            device(x, y, hold(j), 1),
        )

    for s in FAR_MATRICES:
        if s:
            term_copy(s).start()

    @pl.when(jnp.logical_not(holder))
    def _():
        term_copy(0).start()

    @pl.when(holder)
    def _():
        parts[z, 1] = terms[near]
        rows[0, place] = jnp.zeros_like(rows[0, 0])
        for z_ in range(NZ):
            for c in range(CORES):
                arrived = remote(
                    terms.at[0],
                    parts.at[z_, c],
                    term_send.at[0],
                    term_recv.at[z_, c],
                    device(x, y, z, 0),
                )
                if c == 1 and z_ in [hold(j) for j in range(PODS)]:
                    pl.when(z_ != z)(arrived.wait_recv)
                else:
                    arrived.wait_recv()
        for h in range(2):
            total = parts[h * PODS]
            for k in range(1, PODS):
                total = total + parts[h * PODS + k]
            sums[pl.ds(h * CORES, CORES)] = total
        steering = sums[...].reshape(-1, width).astype(jnp.bfloat16)
        rows[0, place, :, :width] = steering

        to_y = []
        for i, peer in enumerate(along_y):
            mine = rows.at[0, place]
            copy = remote(mine, mine, y_send.at[i], y_recv.at[place], peer)
            copy.start()
            to_y.append(copy)
        def x_copy(i, b):
            via = HANDED.get(b) if i == 2 else None
            source = rows.at[0 if via is None else via + 1, b]
            return remote(
                source,
                rows.at[i + 1, b],
                x_send.at[i, b],
                x_recv.at[i, b],
                along_x[i if via is None else via],
            )

        def pass_on(b):
            if b in HANDED:
                x_copy(HANDED[b], b).wait_recv()
                x_copy(2, b).start()

        for b in range(NY):
            other = rows.at[0, b]
            arrived = remote(other, other, y_send.at[0], y_recv.at[b], along_y[0])
            pl.when(b != place)(arrived.wait_recv)
            x_copy(0, b).start()
            x_copy(1, b).start()
            if b not in HANDED:
                x_copy(2, b).start()
            pass_on(b - LAG)
        for b in range(NY - LAG, NY):
            pass_on(b)

        def total_copy(z_, c):
            return remote(
                sums.at[(z_ // PODS) * CORES + c],
                totals.at[near],
                total_send.at[z_, c],
                total_recv.at[near],
                device(x, y, z_, c),
            )

        for_line(lambda z_, c: total_copy(z_, c).start())
        totals[near] = sums[half * CORES + 1]

        raw[...] = gram_product(rows[0].reshape(-1, wide))
        for i in range(len(along_x)):
            for b in range(NY):
                if HANDED.get(b) != i:
                    x_copy(i, b).wait_recv()
            raw[...] += gram_product(rows[i + 1].reshape(-1, wide))

        down = lax.broadcasted_iota(jnp.int32, (LANES, LANES), 0)
        across = lax.broadcasted_iota(jnp.int32, (LANES, LANES), 1)
        diagonal = raw[:LANES, :LANES]
        for i in range(LANES, wide, LANES):
            diagonal = diagonal + raw[i : i + LANES, i : i + LANES]
        trace = jnp.sum(jnp.where(down == across, diagonal, 0.0), keepdims=True)
        inverse = 1.0 / (jnp.sqrt(trace) + epsilon)
        gram = (raw[...] * (inverse * inverse)).astype(jnp.bfloat16)
        start = (rows[0, place].astype(jnp.float32) * inverse).astype(jnp.bfloat16)
        polynomial = (
            coef_b * gram.astype(jnp.float32) + coef_c * dot(gram, gram)
        ).astype(jnp.bfloat16)

        def step(value):
            return coef_a * value + dot(value.astype(jnp.bfloat16), polynomial)

        def next_gram(value):
            return step(dot(step(value).astype(jnp.bfloat16), gram))

        first = step(start.astype(jnp.float32)).astype(jnp.bfloat16).astype(jnp.float32)
        once = next_gram(first)
        second = coef_a * first + coef_b * once + coef_c * next_gram(once)
        depth = pieces.shape[1]
        for q in range(2 * CORES):
            pieces[q] = second[q * depth : (q + 1) * depth].astype(jnp.bfloat16)

        def final_copy(z_, c):
            return remote(
                pieces.at[(z_ // PODS) * CORES + c],
                finals.at[near],
                final_send.at[z_, c],
                final_recv.at[near],
                device(x, y, z_, c),
            )

        for_line(lambda z_, c: final_copy(z_, c).start())
        finals[near] = pieces[half * CORES + 1]
        for copy in to_y:
            copy.wait_send()
        for i in range(len(along_x)):
            for b in range(NY):
                x_copy(i, b).wait_send()
        for_line(lambda z_, c: total_copy(z_, c).wait_send())
        for_line(lambda z_, c: final_copy(z_, c).wait_send())

    def await_matrices(buffer, sem):
        for j in range(PODS):
            arrived = remote(
                buffer.at[j], buffer.at[j], term_send.at[0], sem.at[j], device(x, y, z, 1 - core)
            )
            pl.when(jnp.logical_not(jnp.logical_and(holder, near == j)))(arrived.wait_recv)

    await_matrices(totals, total_recv)
    await_matrices(finals, final_recv)
    for s in FAR_MATRICES:
        if s:
            term_copy(s).wait_send()

    @pl.when(jnp.logical_not(holder))
    def _():
        term_copy(0).wait_send()


def per_device(grads, momentum):
    _, count, depth, width = grads.shape
    wide = -(-width // LANES) * LANES
    height = depth * NX * 2 * NY * CORES
    scale = 0.2 * math.sqrt(max(height, width))
    half, single = jnp.bfloat16, jnp.float32
    dma = pltpu.SemaphoreType.DMA
    totals, finals = pl.pallas_call(
        kernel,
        out_shape=[
            jax.ShapeDtypeStruct(momentum.shape, single),
            jax.ShapeDtypeStruct((count, depth, wide), half),
        ],
        in_specs=[pl.BlockSpec(memory_space=pltpu.HBM)] * 2,
        out_specs=[pl.BlockSpec(memory_space=pltpu.VMEM)] * 2,
        scratch_shapes=[
            pltpu.VMEM((count, depth, width), single),
            pltpu.VMEM((count, depth, width), single),
            pltpu.VMEM((count, depth, width), single),
            pltpu.VMEM((NZ, CORES, depth, width), single),
            pltpu.VMEM((2 * CORES, depth, width), single),
            pltpu.VMEM((NX, NY, 2 * CORES * depth, wide), half),
            pltpu.VMEM((wide, wide), single),
            pltpu.VMEM((2 * CORES, depth, wide), half),
            dma((2,)),
            dma((PODS,)),
            dma((NZ, CORES)),
            dma((NY - 1,)),
            dma((NY,)),
            dma((NX - 1, NY)),
            dma((NX - 1, NY)),
            dma((NZ, CORES)),
            dma((PODS,)),
            dma((NZ, CORES)),
            dma((PODS,)),
        ],
        compiler_params=pltpu.CompilerParams(
            collective_id=0, has_side_effects=True, vmem_limit_bytes=VMEM_LIMIT
        ),
    )(
        pltpu.with_memory_space_constraint(grads, pltpu.HBM),
        pltpu.with_memory_space_constraint(momentum, pltpu.HBM),
    )
    momentum_new = (1 / (1 + momentum_rate)) * totals + (
        momentum_rate - momentum_rate * momentum_rate / (1 + momentum_rate)
    ) * momentum
    return momentum_new, scale * finals[:, :, :width].astype(single)


def solution(mesh):
    in_specs = (P("outer", None, "dp", None), P(None, "dp", None))
    out_specs = (P(None, "dp", None), P(None, "dp", None))
    return jax.shard_map(
        per_device, mesh=mesh, in_specs=in_specs, out_specs=out_specs, check_vma=False
    )
```

```python
import functools
import math

import jax
import jax.numpy as jnp
from jax import lax
from jax.experimental import pallas as pl
from jax.experimental.pallas import tpu as pltpu
from jax.sharding import PartitionSpec as P

MESH = pl.DeviceIdType.MESH

coef_a = 3.4445
coef_b = -4.775
coef_c = 2.0315
momentum_rate = 0.95
epsilon = 1e-06

PODS = 6
NZ = 12
NX = 4
NY = 8
CORES = 2
LANES = 128
HOLDERS = (0, 2, 3, 5, 8, 10)
VMEM_LIMIT = 24 << 20
ALONG_Y = (4, 3, 5, 2, 6, 1, 7)
ALONG_X = (1, 3, 2)
HANDED = {0: 0, 1: 1, 2: 0, 3: 1, 4: 0, 5: 1, 6: 0}
LAG = 4
FAR_MATRICES = (3, 2, 4, 1, 5, 0)


def hold(j):
    if isinstance(j, int):
        return HOLDERS[j]
    return sum(jnp.where(j == k, HOLDERS[k], 0) for k in range(PODS))


def slot(y):
    return jnp.where(y < NY // 2, y, 3 * NY // 2 - 1 - y)


def dot(left, right):
    return jnp.dot(left, right, preferred_element_type=jnp.float32)


def gram_product(matrix):
    return lax.dot_general(
        matrix, matrix, (((0,), (0,)), ((), ())), preferred_element_type=jnp.float32
    )


def kernel(
    grads,
    momentum,
    totals,
    finals,
    my_grads,
    my_momentum,
    terms,
    parts,
    sums,
    rows,
    raw,
    pieces,
    local_sem,
    term_send,
    term_recv,
    y_send,
    y_recv,
    x_send,
    x_recv,
    total_send,
    total_recv,
    final_send,
    final_recv,
):
    width = grads.shape[-1]
    wide = rows.shape[-1]
    pod = lax.axis_index("outer")
    dp = lax.axis_index("dp")
    core = lax.rem(dp, 2)
    y = lax.rem(dp // 2, NY)
    half = lax.rem(dp // (2 * NY), 2)
    x = dp // (4 * NY)
    z = half * PODS + pod
    near = sum(jnp.where(z == HOLDERS[k], k, 0) for k in range(PODS))
    holder = jnp.logical_and(core == 1, hold(near) == z)
    near = jnp.where(hold(near) == z, near, z // 2)
    place = slot(y)

    def device(x_, y_, z_, core_):
        return (lax.rem(z_, PODS), ((x_ * 2 + z_ // PODS) * NY + y_) * 2 + core_)

    def remote(source, target, send_sem, recv_sem, peer):
        return pltpu.make_async_remote_copy(
            src_ref=source,
            dst_ref=target,
            send_sem=send_sem,
            recv_sem=recv_sem,
            device_id=peer,
            device_id_type=MESH,
        )

    def for_line(act):
        for z_ in range(NZ):
            for c in (1, 0):
                if c == 1 and z_ in [hold(j) for j in range(PODS)]:
                    pl.when(z_ != z)(functools.partial(act, z_, c))
                else:
                    act(z_, c)

    load_grads = pltpu.make_async_copy(grads.at[0], my_grads, local_sem.at[0])
    load_momentum = pltpu.make_async_copy(momentum, my_momentum, local_sem.at[1])
    load_grads.start()
    load_momentum.start()

    along_y = [device(x, lax.rem(y + k, NY), z, 1) for k in ALONG_Y]
    along_x = [device(lax.rem(x + k, NX), y, z, 1) for k in ALONG_X]
    targets = {}
    for s in FAR_MATRICES:
        j = lax.rem(near + s, PODS)
        targets[s] = (j, device(x, y, hold(j), 1))
    barrier = pltpu.get_barrier_semaphore()

    def greet(peer):
        pl.semaphore_signal(barrier, inc=1, device_id=peer, device_id_type=MESH)

    @pl.when(holder)
    def _():
        for d in (6, 5, 7, 4, 8, 3, 9, 2, 10, 1, 11, 0):
            for c in range(CORES):
                if (d, c) != (0, 1):
                    greet(device(x, y, lax.rem(z + d, NZ), c))
        for peer in along_y + along_x:
            greet(peer)

    @pl.when(jnp.logical_not(holder))
    def _():
        for s in FAR_MATRICES:
            greet(targets[s][1])

    load_grads.wait()
    load_momentum.wait()
    terms[...] = (1 + momentum_rate) * my_grads[...] + (
        momentum_rate * momentum_rate / PODS
    ) * my_momentum[...]

    @pl.when(holder)
    def _():
        pl.semaphore_wait(barrier, NZ * CORES - 1 + len(along_y) + len(along_x))

    @pl.when(jnp.logical_not(holder))
    def _():
        pl.semaphore_wait(barrier, PODS)

    def term_copy(s):
        j, peer = targets[s]
        return remote(
            terms.at[j],
            parts.at[z, core],
            term_send.at[s],
            term_recv.at[z, core],
            peer,
        )

    for s in FAR_MATRICES:
        if s:
            term_copy(s).start()

    @pl.when(jnp.logical_not(holder))
    def _():
        term_copy(0).start()

    @pl.when(holder)
    def _():
        parts[z, 1] = terms[near]
        rows[0, place] = jnp.zeros_like(rows[0, 0])
        for z_ in range(NZ):
            for c in range(CORES):
                arrived = remote(
                    terms.at[0],
                    parts.at[z_, c],
                    term_send.at[0],
                    term_recv.at[z_, c],
                    device(x, y, z, 0),
                )
                if c == 1 and z_ in [hold(j) for j in range(PODS)]:
                    pl.when(z_ != z)(arrived.wait_recv)
                else:
                    arrived.wait_recv()
        for h in range(2):
            total = parts[h * PODS]
            for k in range(1, PODS):
                total = total + parts[h * PODS + k]
            sums[pl.ds(h * CORES, CORES)] = total
        steering = sums[...].reshape(-1, width).astype(jnp.bfloat16)
        rows[0, place, :, :width] = steering

        to_y = []
        for i, peer in enumerate(along_y):
            mine = rows.at[0, place]
            copy = remote(mine, mine, y_send.at[i], y_recv.at[place], peer)
            copy.start()
            to_y.append(copy)
        def x_copy(i, b):
            via = HANDED.get(b) if i == 2 else None
            source = rows.at[0 if via is None else via + 1, b]
            return remote(
                source,
                rows.at[i + 1, b],
                x_send.at[i, b],
                x_recv.at[i, b],
                along_x[i if via is None else via],
            )

        def pass_on(b):
            if b in HANDED:
                x_copy(HANDED[b], b).wait_recv()
                x_copy(2, b).start()

        for b in range(NY):
            other = rows.at[0, b]
            arrived = remote(other, other, y_send.at[0], y_recv.at[b], along_y[0])
            pl.when(b != place)(arrived.wait_recv)
            x_copy(0, b).start()
            x_copy(1, b).start()
            if b not in HANDED:
                x_copy(2, b).start()
            pass_on(b - LAG)
        for b in range(NY - LAG, NY):
            pass_on(b)

        def total_copy(z_, c):
            return remote(
                sums.at[(z_ // PODS) * CORES + c],
                totals.at[near],
                total_send.at[z_, c],
                total_recv.at[near],
                device(x, y, z_, c),
            )

        for_line(lambda z_, c: total_copy(z_, c).start())
        totals[near] = sums[half * CORES + 1]

        raw[...] = gram_product(rows[0].reshape(-1, wide))
        for i in range(len(along_x)):
            for b in range(NY):
                if HANDED.get(b) != i:
                    x_copy(i, b).wait_recv()
            raw[...] += gram_product(rows[i + 1].reshape(-1, wide))

        down = lax.broadcasted_iota(jnp.int32, (LANES, LANES), 0)
        across = lax.broadcasted_iota(jnp.int32, (LANES, LANES), 1)
        diagonal = raw[:LANES, :LANES]
        for i in range(LANES, wide, LANES):
            diagonal = diagonal + raw[i : i + LANES, i : i + LANES]
        trace = jnp.sum(jnp.where(down == across, diagonal, 0.0), keepdims=True)
        inverse = 1.0 / (jnp.sqrt(trace) + epsilon)
        gram = (raw[...] * (inverse * inverse)).astype(jnp.bfloat16)
        start = (rows[0, place].astype(jnp.float32) * inverse).astype(jnp.bfloat16)
        polynomial = (
            coef_b * gram.astype(jnp.float32) + coef_c * dot(gram, gram)
        ).astype(jnp.bfloat16)

        def step(value):
            return coef_a * value + dot(value.astype(jnp.bfloat16), polynomial)

        def next_gram(value):
            return step(dot(step(value).astype(jnp.bfloat16), gram))

        first = step(start.astype(jnp.float32)).astype(jnp.bfloat16).astype(jnp.float32)
        once = next_gram(first)
        second = coef_a * first + coef_b * once + coef_c * next_gram(once)
        depth = pieces.shape[1]
        for q in range(2 * CORES):
            pieces[q] = second[q * depth : (q + 1) * depth].astype(jnp.bfloat16)

        def final_copy(z_, c):
            return remote(
                pieces.at[(z_ // PODS) * CORES + c],
                finals.at[near],
                final_send.at[z_, c],
                final_recv.at[near],
                device(x, y, z_, c),
            )

        for_line(lambda z_, c: final_copy(z_, c).start())
        finals[near] = pieces[half * CORES + 1]
        for copy in to_y:
            copy.wait_send()
        for i in range(len(along_x)):
            for b in range(NY):
                x_copy(i, b).wait_send()
        for_line(lambda z_, c: total_copy(z_, c).wait_send())
        for_line(lambda z_, c: final_copy(z_, c).wait_send())

    def await_matrices(buffer, sem):
        for j in range(PODS):
            arrived = remote(
                buffer.at[j], buffer.at[j], term_send.at[0], sem.at[j], device(x, y, z, 1 - core)
            )
            pl.when(jnp.logical_not(jnp.logical_and(holder, near == j)))(arrived.wait_recv)

    await_matrices(totals, total_recv)
    await_matrices(finals, final_recv)
    for s in FAR_MATRICES:
        if s:
            term_copy(s).wait_send()

    @pl.when(jnp.logical_not(holder))
    def _():
        term_copy(0).wait_send()


def finish(scale, totals, finals, momentum, momentum_out, update_out, first, second, sem):
    store_update = pltpu.make_async_copy(first, update_out, sem.at[0])
    store_momentum = pltpu.make_async_copy(second, momentum_out, sem.at[1])
    first[...] = scale * finals[:, :, : first.shape[-1]].astype(jnp.float32)
    store_update.start()
    second[...] = (1 / (1 + momentum_rate)) * totals[...] + (
        momentum_rate - momentum_rate * momentum_rate / (1 + momentum_rate)
    ) * momentum[...]
    store_momentum.start()
    store_update.wait()
    store_momentum.wait()


def per_device(grads, momentum):
    _, count, depth, width = grads.shape
    wide = -(-width // LANES) * LANES
    height = depth * NX * 2 * NY * CORES
    scale = 0.2 * math.sqrt(max(height, width))
    half, single = jnp.bfloat16, jnp.float32
    dma = pltpu.SemaphoreType.DMA
    totals, finals = pl.pallas_call(
        kernel,
        out_shape=[
            jax.ShapeDtypeStruct(momentum.shape, single),
            jax.ShapeDtypeStruct((count, depth, wide), half),
        ],
        in_specs=[pl.BlockSpec(memory_space=pltpu.HBM)] * 2,
        out_specs=[pl.BlockSpec(memory_space=pltpu.VMEM)] * 2,
        scratch_shapes=[
            pltpu.VMEM((count, depth, width), single),
            pltpu.VMEM((count, depth, width), single),
            pltpu.VMEM((count, depth, width), single),
            pltpu.VMEM((NZ, CORES, depth, width), single),
            pltpu.VMEM((2 * CORES, depth, width), single),
            pltpu.VMEM((NX, NY, 2 * CORES * depth, wide), half),
            pltpu.VMEM((wide, wide), single),
            pltpu.VMEM((2 * CORES, depth, wide), half),
            dma((2,)),
            dma((PODS,)),
            dma((NZ, CORES)),
            dma((NY - 1,)),
            dma((NY,)),
            dma((NX - 1, NY)),
            dma((NX - 1, NY)),
            dma((NZ, CORES)),
            dma((PODS,)),
            dma((NZ, CORES)),
            dma((PODS,)),
        ],
        compiler_params=pltpu.CompilerParams(
            collective_id=0, has_side_effects=True, vmem_limit_bytes=VMEM_LIMIT
        ),
    )(
        pltpu.with_memory_space_constraint(grads, pltpu.HBM),
        pltpu.with_memory_space_constraint(momentum, pltpu.HBM),
    )
    return pl.pallas_call(
        functools.partial(finish, scale),
        out_shape=[jax.ShapeDtypeStruct(momentum.shape, single)] * 2,
        in_specs=[pl.BlockSpec(memory_space=pltpu.VMEM)] * 3,
        out_specs=[pl.BlockSpec(memory_space=pltpu.HBM)] * 2,
        scratch_shapes=[
            pltpu.VMEM(momentum.shape, single),
            pltpu.VMEM(momentum.shape, single),
            dma((2,)),
        ],
        compiler_params=pltpu.CompilerParams(vmem_limit_bytes=VMEM_LIMIT),
    )(totals, finals, momentum)


def solution(mesh):
    in_specs = (P("outer", None, "dp", None), P(None, "dp", None))
    out_specs = (P(None, "dp", None), P(None, "dp", None))
    return jax.shard_map(
        per_device, mesh=mesh, in_specs=in_specs, out_specs=out_specs, check_vma=False
    )
```

```python
import functools
import math

import jax
import jax.numpy as jnp
from jax import lax
from jax.experimental import pallas as pl
from jax.experimental.pallas import tpu as pltpu
from jax.sharding import PartitionSpec as P

MESH = pl.DeviceIdType.MESH

coef_a = 3.4445
coef_b = -4.775
coef_c = 2.0315
momentum_rate = 0.95
epsilon = 1e-06

PODS = 6
NZ = 12
NX = 4
NY = 8
CORES = 2
LANES = 128
HOLDERS = (0, 1, 3, 5, 9, 10)
VMEM_LIMIT = 24 << 20
ALONG_Y = (4, 5, 3, 6, 2, 7, 1)
ALONG_X = (1, 3, 2)
HANDED = {0: 0, 1: 1, 2: 0, 3: 1, 4: 0, 5: 1, 6: 0}
LAG = 4
FAR_MATRICES = (3, 4, 2, 5, 1, 0)


def hold(j):
    if isinstance(j, int):
        return HOLDERS[j]
    return sum(jnp.where(j == k, HOLDERS[k], 0) for k in range(PODS))


def slot(y):
    return jnp.where(y < NY // 2, y, 3 * NY // 2 - 1 - y)


def dot(left, right):
    return jnp.dot(left, right, preferred_element_type=jnp.float32)


def gram_product(matrix):
    return lax.dot_general(
        matrix, matrix, (((0,), (0,)), ((), ())), preferred_element_type=jnp.float32
    )


def kernel(
    grads,
    momentum,
    totals,
    finals,
    my_grads,
    my_momentum,
    terms,
    parts,
    sums,
    rows,
    raw,
    pieces,
    local_sem,
    term_send,
    term_recv,
    y_send,
    y_recv,
    x_send,
    x_recv,
    total_send,
    total_recv,
    final_send,
    final_recv,
):
    width = grads.shape[-1]
    wide = rows.shape[-1]
    pod = lax.axis_index("outer")
    dp = lax.axis_index("dp")
    core = lax.rem(dp, 2)
    y = lax.rem(dp // 2, NY)
    half = lax.rem(dp // (2 * NY), 2)
    x = dp // (4 * NY)
    z = half * PODS + pod
    near = sum(jnp.where(z == HOLDERS[k], k, 0) for k in range(PODS))
    holder = jnp.logical_and(core == 1, hold(near) == z)
    near = jnp.where(hold(near) == z, near, z // 2)
    place = slot(y)

    def device(x_, y_, z_, core_):
        return (lax.rem(z_, PODS), ((x_ * 2 + z_ // PODS) * NY + y_) * 2 + core_)

    def remote(source, target, send_sem, recv_sem, peer):
        return pltpu.make_async_remote_copy(
            src_ref=source,
            dst_ref=target,
            send_sem=send_sem,
            recv_sem=recv_sem,
            device_id=peer,
            device_id_type=MESH,
        )

    def for_line(act):
        for z_ in range(NZ):
            for c in (1, 0):
                if c == 1 and z_ in [hold(j) for j in range(PODS)]:
                    pl.when(z_ != z)(functools.partial(act, z_, c))
                else:
                    act(z_, c)

    load_grads = pltpu.make_async_copy(grads.at[0], my_grads, local_sem.at[0])
    load_momentum = pltpu.make_async_copy(momentum, my_momentum, local_sem.at[1])
    load_grads.start()
    load_momentum.start()

    along_y = [device(x, lax.rem(y + k, NY), z, 1) for k in ALONG_Y]
    along_x = [device(lax.rem(x + k, NX), y, z, 1) for k in ALONG_X]
    targets = {}
    for s in FAR_MATRICES:
        j = lax.rem(near + s, PODS)
        targets[s] = (j, device(x, y, hold(j), 1))
    barrier = pltpu.get_barrier_semaphore()

    def greet(peer):
        pl.semaphore_signal(barrier, inc=1, device_id=peer, device_id_type=MESH)

    @pl.when(holder)
    def _():
        for d in (6, 5, 7, 4, 8, 3, 9, 2, 10, 1, 11, 0):
            for c in range(CORES):
                if (d, c) != (0, 1):
                    greet(device(x, y, lax.rem(z + d, NZ), c))
        for peer in along_y + along_x:
            greet(peer)

    @pl.when(jnp.logical_not(holder))
    def _():
        for s in FAR_MATRICES:
            greet(targets[s][1])

    load_grads.wait()
    load_momentum.wait()
    terms[...] = (1 + momentum_rate) * my_grads[...] + (
        momentum_rate * momentum_rate / PODS
    ) * my_momentum[...]

    @pl.when(holder)
    def _():
        pl.semaphore_wait(barrier, NZ * CORES - 1 + len(along_y) + len(along_x))

    @pl.when(jnp.logical_not(holder))
    def _():
        pl.semaphore_wait(barrier, PODS)

    def term_copy(s):
        j, peer = targets[s]
        return remote(
            terms.at[j],
            parts.at[z, core],
            term_send.at[s],
            term_recv.at[z, core],
            peer,
        )

    for s in FAR_MATRICES:
        if s:
            term_copy(s).start()

    @pl.when(jnp.logical_not(holder))
    def _():
        term_copy(0).start()

    @pl.when(holder)
    def _():
        parts[z, 1] = terms[near]
        rows[0, place] = jnp.zeros_like(rows[0, 0])
        for z_ in range(NZ):
            for c in range(CORES):
                arrived = remote(
                    terms.at[0],
                    parts.at[z_, c],
                    term_send.at[0],
                    term_recv.at[z_, c],
                    device(x, y, z, 0),
                )
                if c == 1 and z_ in [hold(j) for j in range(PODS)]:
                    pl.when(z_ != z)(arrived.wait_recv)
                else:
                    arrived.wait_recv()
        for h in range(2):
            total = parts[h * PODS]
            for k in range(1, PODS):
                total = total + parts[h * PODS + k]
            sums[pl.ds(h * CORES, CORES)] = total
        steering = sums[...].reshape(-1, width).astype(jnp.bfloat16)
        rows[0, place, :, :width] = steering

        to_y = []
        for i, peer in enumerate(along_y):
            mine = rows.at[0, place]
            copy = remote(mine, mine, y_send.at[i], y_recv.at[place], peer)
            copy.start()
            to_y.append(copy)
        def x_copy(i, b):
            via = HANDED.get(b) if i == 2 else None
            source = rows.at[0 if via is None else via + 1, b]
            return remote(
                source,
                rows.at[i + 1, b],
                x_send.at[i, b],
                x_recv.at[i, b],
                along_x[i if via is None else via],
            )

        def pass_on(b):
            if b in HANDED:
                x_copy(HANDED[b], b).wait_recv()
                x_copy(2, b).start()

        def send_x(b):
            x_copy(0, b).start()
            x_copy(1, b).start()
            if b not in HANDED:
                x_copy(2, b).start()

        for b in range(NY):
            pl.when(b == place)(functools.partial(send_x, b))

        def relay(b):
            other = rows.at[0, b]
            remote(other, other, y_send.at[0], y_recv.at[b], along_y[0]).wait_recv()
            send_x(b)

        for b in range(NY):
            pl.when(b != place)(functools.partial(relay, b))
            pass_on(b - LAG)
        for b in range(NY - LAG, NY):
            pass_on(b)

        def total_copy(z_, c):
            return remote(
                sums.at[(z_ // PODS) * CORES + c],
                totals.at[near],
                total_send.at[z_, c],
                total_recv.at[near],
                device(x, y, z_, c),
            )

        for_line(lambda z_, c: total_copy(z_, c).start())
        totals[near] = sums[half * CORES + 1]

        raw[...] = gram_product(rows[0].reshape(-1, wide))
        for i in range(len(along_x)):
            for b in range(NY):
                if HANDED.get(b) != i:
                    x_copy(i, b).wait_recv()
            raw[...] += gram_product(rows[i + 1].reshape(-1, wide))

        down = lax.broadcasted_iota(jnp.int32, (LANES, LANES), 0)
        across = lax.broadcasted_iota(jnp.int32, (LANES, LANES), 1)
        diagonal = raw[:LANES, :LANES]
        for i in range(LANES, wide, LANES):
            diagonal = diagonal + raw[i : i + LANES, i : i + LANES]
        trace = jnp.sum(jnp.where(down == across, diagonal, 0.0), keepdims=True)
        inverse = 1.0 / (jnp.sqrt(trace) + epsilon)
        gram = (raw[...] * (inverse * inverse)).astype(jnp.bfloat16)
        start = (rows[0, place].astype(jnp.float32) * inverse).astype(jnp.bfloat16)
        polynomial = (
            coef_b * gram.astype(jnp.float32) + coef_c * dot(gram, gram)
        ).astype(jnp.bfloat16)

        def step(value):
            return coef_a * value + dot(value.astype(jnp.bfloat16), polynomial)

        def next_gram(value):
            return step(dot(step(value).astype(jnp.bfloat16), gram))

        first = step(start.astype(jnp.float32)).astype(jnp.bfloat16).astype(jnp.float32)
        once = next_gram(first)
        second = coef_a * first + coef_b * once + coef_c * next_gram(once)
        depth = pieces.shape[1]
        for q in range(2 * CORES):
            pieces[q] = second[q * depth : (q + 1) * depth].astype(jnp.bfloat16)

        def final_copy(z_, c):
            return remote(
                pieces.at[(z_ // PODS) * CORES + c],
                finals.at[near],
                final_send.at[z_, c],
                final_recv.at[near],
                device(x, y, z_, c),
            )

        for_line(lambda z_, c: final_copy(z_, c).start())
        finals[near] = pieces[half * CORES + 1]
        for copy in to_y:
            copy.wait_send()
        for i in range(len(along_x)):
            for b in range(NY):
                x_copy(i, b).wait_send()
        for_line(lambda z_, c: total_copy(z_, c).wait_send())
        for_line(lambda z_, c: final_copy(z_, c).wait_send())

    def await_matrices(buffer, sem):
        for j in range(PODS):
            arrived = remote(
                buffer.at[j], buffer.at[j], term_send.at[0], sem.at[j], device(x, y, z, 1 - core)
            )
            pl.when(jnp.logical_not(jnp.logical_and(holder, near == j)))(arrived.wait_recv)

    await_matrices(totals, total_recv)
    await_matrices(finals, final_recv)
    for s in FAR_MATRICES:
        if s:
            term_copy(s).wait_send()

    @pl.when(jnp.logical_not(holder))
    def _():
        term_copy(0).wait_send()


def finish(scale, totals, finals, momentum, momentum_out, update_out, first, second, sem):
    store_update = pltpu.make_async_copy(first, update_out, sem.at[0])
    store_momentum = pltpu.make_async_copy(second, momentum_out, sem.at[1])
    first[...] = scale * finals[:, :, : first.shape[-1]].astype(jnp.float32)
    store_update.start()
    second[...] = (1 / (1 + momentum_rate)) * totals[...] + (
        momentum_rate - momentum_rate * momentum_rate / (1 + momentum_rate)
    ) * momentum[...]
    store_momentum.start()
    store_update.wait()
    store_momentum.wait()


def per_device(grads, momentum):
    _, count, depth, width = grads.shape
    wide = -(-width // LANES) * LANES
    height = depth * NX * 2 * NY * CORES
    scale = 0.2 * math.sqrt(max(height, width))
    half, single = jnp.bfloat16, jnp.float32
    dma = pltpu.SemaphoreType.DMA
    totals, finals = pl.pallas_call(
        kernel,
        out_shape=[
            jax.ShapeDtypeStruct(momentum.shape, single),
            jax.ShapeDtypeStruct((count, depth, wide), half),
        ],
        in_specs=[pl.BlockSpec(memory_space=pltpu.HBM)] * 2,
        out_specs=[pl.BlockSpec(memory_space=pltpu.VMEM)] * 2,
        scratch_shapes=[
            pltpu.VMEM((count, depth, width), single),
            pltpu.VMEM((count, depth, width), single),
            pltpu.VMEM((count, depth, width), single),
            pltpu.VMEM((NZ, CORES, depth, width), single),
            pltpu.VMEM((2 * CORES, depth, width), single),
            pltpu.VMEM((NX, NY, 2 * CORES * depth, wide), half),
            pltpu.VMEM((wide, wide), single),
            pltpu.VMEM((2 * CORES, depth, wide), half),
            dma((2,)),
            dma((PODS,)),
            dma((NZ, CORES)),
            dma((NY - 1,)),
            dma((NY,)),
            dma((NX - 1, NY)),
            dma((NX - 1, NY)),
            dma((NZ, CORES)),
            dma((PODS,)),
            dma((NZ, CORES)),
            dma((PODS,)),
        ],
        compiler_params=pltpu.CompilerParams(
            collective_id=0, has_side_effects=True, vmem_limit_bytes=VMEM_LIMIT
        ),
    )(
        pltpu.with_memory_space_constraint(grads, pltpu.HBM),
        pltpu.with_memory_space_constraint(momentum, pltpu.HBM),
    )
    return pl.pallas_call(
        functools.partial(finish, scale),
        out_shape=[jax.ShapeDtypeStruct(momentum.shape, single)] * 2,
        in_specs=[pl.BlockSpec(memory_space=pltpu.VMEM)] * 3,
        out_specs=[pl.BlockSpec(memory_space=pltpu.HBM)] * 2,
        scratch_shapes=[
            pltpu.VMEM(momentum.shape, single),
            pltpu.VMEM(momentum.shape, single),
            dma((2,)),
        ],
        compiler_params=pltpu.CompilerParams(vmem_limit_bytes=VMEM_LIMIT),
    )(totals, finals, momentum)


def solution(mesh):
    in_specs = (P("outer", None, "dp", None), P(None, "dp", None))
    out_specs = (P(None, "dp", None), P(None, "dp", None))
    return jax.shard_map(
        per_device, mesh=mesh, in_specs=in_specs, out_specs=out_specs, check_vma=False
    )
```

```python
import functools
import math

import jax
import jax.numpy as jnp
from jax import lax
from jax.experimental import pallas as pl
from jax.experimental.pallas import tpu as pltpu
from jax.sharding import PartitionSpec as P

MESH = pl.DeviceIdType.MESH

coef_a = 3.4445
coef_b = -4.775
coef_c = 2.0315
momentum_rate = 0.95
epsilon = 1e-06

PODS = 6
NZ = 12
NX = 4
NY = 8
CORES = 2
LANES = 128
HOLDERS = (0, 1, 3, 5, 9, 10)
VMEM_LIMIT = 24 << 20
ALONG_Y = (4, 5, 3, 6, 2, 7, 1)
ALONG_X = (1, 3, 2)
HANDED = {0: 0, 1: 1, 2: 0, 3: 1, 4: 0, 5: 1, 6: 0, 7: 1}
LAG = 4
FAR_MATRICES = (3, 4, 2, 5, 1, 0)


def hold(j):
    if isinstance(j, int):
        return HOLDERS[j]
    return sum(jnp.where(j == k, HOLDERS[k], 0) for k in range(PODS))


def slot(y):
    return jnp.where(y < NY // 2, y, 3 * NY // 2 - 1 - y)


def dot(left, right):
    return jnp.dot(left, right, preferred_element_type=jnp.float32)


def gram_product(matrix):
    return lax.dot_general(
        matrix, matrix, (((0,), (0,)), ((), ())), preferred_element_type=jnp.float32
    )


def kernel(
    grads,
    momentum,
    totals,
    finals,
    my_grads,
    my_momentum,
    terms,
    parts,
    sums,
    rows,
    raw,
    pieces,
    local_sem,
    term_send,
    term_recv,
    y_send,
    y_recv,
    x_send,
    x_recv,
    total_send,
    total_recv,
    final_send,
    final_recv,
):
    width = grads.shape[-1]
    wide = rows.shape[-1]
    pod = lax.axis_index("outer")
    dp = lax.axis_index("dp")
    core = lax.rem(dp, 2)
    y = lax.rem(dp // 2, NY)
    half = lax.rem(dp // (2 * NY), 2)
    x = dp // (4 * NY)
    z = half * PODS + pod
    near = sum(jnp.where(z == HOLDERS[k], k, 0) for k in range(PODS))
    holder = jnp.logical_and(core == 1, hold(near) == z)
    near = jnp.where(hold(near) == z, near, z // 2)
    place = slot(y)

    def device(x_, y_, z_, core_):
        return (lax.rem(z_, PODS), ((x_ * 2 + z_ // PODS) * NY + y_) * 2 + core_)

    def remote(source, target, send_sem, recv_sem, peer):
        return pltpu.make_async_remote_copy(
            src_ref=source,
            dst_ref=target,
            send_sem=send_sem,
            recv_sem=recv_sem,
            device_id=peer,
            device_id_type=MESH,
        )

    def for_line(act):
        for z_ in range(NZ):
            for c in (1, 0):
                if c == 1 and z_ in [hold(j) for j in range(PODS)]:
                    pl.when(z_ != z)(functools.partial(act, z_, c))
                else:
                    act(z_, c)

    load_grads = pltpu.make_async_copy(grads.at[0], my_grads, local_sem.at[0])
    load_momentum = pltpu.make_async_copy(momentum, my_momentum, local_sem.at[1])
    load_grads.start()
    load_momentum.start()

    along_y = [device(x, lax.rem(y + k, NY), z, 1) for k in ALONG_Y]
    along_x = [device(lax.rem(x + k, NX), y, z, 1) for k in ALONG_X]
    targets = {}
    for s in FAR_MATRICES:
        j = lax.rem(near + s, PODS)
        targets[s] = (j, device(x, y, hold(j), 1))
    barrier = pltpu.get_barrier_semaphore()

    def greet(peer):
        pl.semaphore_signal(barrier, inc=1, device_id=peer, device_id_type=MESH)

    @pl.when(holder)
    def _():
        for d in (6, 5, 7, 4, 8, 3, 9, 2, 10, 1, 11, 0):
            for c in range(CORES):
                if (d, c) != (0, 1):
                    greet(device(x, y, lax.rem(z + d, NZ), c))
        for peer in along_y + along_x:
            greet(peer)

    @pl.when(jnp.logical_not(holder))
    def _():
        for s in FAR_MATRICES:
            greet(targets[s][1])

    load_grads.wait()
    load_momentum.wait()
    terms[...] = (1 + momentum_rate) * my_grads[...] + (
        momentum_rate * momentum_rate / PODS
    ) * my_momentum[...]

    @pl.when(holder)
    def _():
        pl.semaphore_wait(barrier, NZ * CORES - 1 + len(along_y) + len(along_x))

    @pl.when(jnp.logical_not(holder))
    def _():
        pl.semaphore_wait(barrier, PODS)

    def term_copy(s):
        j, peer = targets[s]
        return remote(
            terms.at[j],
            parts.at[z, core],
            term_send.at[s],
            term_recv.at[z, core],
            peer,
        )

    for s in FAR_MATRICES:
        if s:
            term_copy(s).start()

    @pl.when(jnp.logical_not(holder))
    def _():
        term_copy(0).start()

    @pl.when(holder)
    def _():
        parts[z, 1] = terms[near]
        rows[0, place] = jnp.zeros_like(rows[0, 0])
        for z_ in range(NZ):
            for c in range(CORES):
                arrived = remote(
                    terms.at[0],
                    parts.at[z_, c],
                    term_send.at[0],
                    term_recv.at[z_, c],
                    device(x, y, z, 0),
                )
                if c == 1 and z_ in [hold(j) for j in range(PODS)]:
                    pl.when(z_ != z)(arrived.wait_recv)
                else:
                    arrived.wait_recv()
        for h in range(2):
            total = parts[h * PODS]
            for k in range(1, PODS):
                total = total + parts[h * PODS + k]
            sums[pl.ds(h * CORES, CORES)] = total
        steering = sums[...].reshape(-1, width).astype(jnp.bfloat16)
        rows[0, place, :, :width] = steering

        to_y = []
        for i, peer in enumerate(along_y):
            mine = rows.at[0, place]
            copy = remote(mine, mine, y_send.at[i], y_recv.at[place], peer)
            copy.start()
            to_y.append(copy)
        def x_copy(i, b):
            via = HANDED.get(b) if i == 2 else None
            source = rows.at[0 if via is None else via + 1, b]
            return remote(
                source,
                rows.at[i + 1, b],
                x_send.at[i, b],
                x_recv.at[i, b],
                along_x[i if via is None else via],
            )

        def pass_on(b):
            if b in HANDED:
                x_copy(HANDED[b], b).wait_recv()
                x_copy(2, b).start()

        def send_x(b):
            x_copy(0, b).start()
            x_copy(1, b).start()
            if b not in HANDED:
                x_copy(2, b).start()

        for b in range(NY):
            pl.when(b == place)(functools.partial(send_x, b))

        def relay(b):
            other = rows.at[0, b]
            remote(other, other, y_send.at[0], y_recv.at[b], along_y[0]).wait_recv()
            send_x(b)

        for b in range(NY):
            pl.when(b != place)(functools.partial(relay, b))
            pass_on(b - LAG)
        for b in range(NY - LAG, NY):
            pass_on(b)

        def total_copy(z_, c):
            return remote(
                sums.at[(z_ // PODS) * CORES + c],
                totals.at[near],
                total_send.at[z_, c],
                total_recv.at[near],
                device(x, y, z_, c),
            )

        for_line(lambda z_, c: total_copy(z_, c).start())
        totals[near] = sums[half * CORES + 1]

        raw[...] = gram_product(rows[0].reshape(-1, wide))
        for i in range(len(along_x)):
            for b in range(NY):
                if HANDED.get(b) != i:
                    x_copy(i, b).wait_recv()
            raw[...] += gram_product(rows[i + 1].reshape(-1, wide))

        down = lax.broadcasted_iota(jnp.int32, (LANES, LANES), 0)
        across = lax.broadcasted_iota(jnp.int32, (LANES, LANES), 1)
        diagonal = raw[:LANES, :LANES]
        for i in range(LANES, wide, LANES):
            diagonal = diagonal + raw[i : i + LANES, i : i + LANES]
        trace = jnp.sum(jnp.where(down == across, diagonal, 0.0), keepdims=True)
        inverse = 1.0 / (jnp.sqrt(trace) + epsilon)
        gram = (raw[...] * (inverse * inverse)).astype(jnp.bfloat16)
        start = (rows[0, place].astype(jnp.float32) * inverse).astype(jnp.bfloat16)
        polynomial = jnp.concatenate(
            [
                (
                    coef_b * gram[:width].astype(jnp.float32) + coef_c * dot(gram[:width], gram)
                ).astype(jnp.bfloat16),
                jnp.zeros((wide - width, wide), jnp.bfloat16),
            ],
            axis=0,
        )

        def step(value):
            return coef_a * value + dot(value.astype(jnp.bfloat16), polynomial)

        def next_gram(value):
            return step(dot(step(value).astype(jnp.bfloat16), gram))

        first = step(start.astype(jnp.float32)).astype(jnp.bfloat16).astype(jnp.float32)
        once = next_gram(first)
        second = coef_a * first + coef_b * once + coef_c * next_gram(once)
        depth = pieces.shape[1]
        for q in range(2 * CORES):
            pieces[q] = second[q * depth : (q + 1) * depth].astype(jnp.bfloat16)

        def final_copy(z_, c):
            return remote(
                pieces.at[(z_ // PODS) * CORES + c],
                finals.at[near],
                final_send.at[z_, c],
                final_recv.at[near],
                device(x, y, z_, c),
            )

        for_line(lambda z_, c: final_copy(z_, c).start())
        finals[near] = pieces[half * CORES + 1]
        for copy in to_y:
            copy.wait_send()
        for i in range(len(along_x)):
            for b in range(NY):
                x_copy(i, b).wait_send()
        for_line(lambda z_, c: total_copy(z_, c).wait_send())
        for_line(lambda z_, c: final_copy(z_, c).wait_send())

    def await_matrices(buffer, sem):
        for j in range(PODS):
            arrived = remote(
                buffer.at[j], buffer.at[j], term_send.at[0], sem.at[j], device(x, y, z, 1 - core)
            )
            pl.when(jnp.logical_not(jnp.logical_and(holder, near == j)))(arrived.wait_recv)

    await_matrices(totals, total_recv)
    await_matrices(finals, final_recv)
    for s in FAR_MATRICES:
        if s:
            term_copy(s).wait_send()

    @pl.when(jnp.logical_not(holder))
    def _():
        term_copy(0).wait_send()


def finish(scale, totals, finals, momentum, momentum_out, update_out, first, second, sem):
    store_update = pltpu.make_async_copy(first, update_out, sem.at[0])
    store_momentum = pltpu.make_async_copy(second, momentum_out, sem.at[1])
    first[...] = scale * finals[:, :, : first.shape[-1]].astype(jnp.float32)
    store_update.start()
    second[...] = (1 / (1 + momentum_rate)) * totals[...] + (
        momentum_rate - momentum_rate * momentum_rate / (1 + momentum_rate)
    ) * momentum[...]
    store_momentum.start()
    store_update.wait()
    store_momentum.wait()


def per_device(grads, momentum):
    _, count, depth, width = grads.shape
    wide = -(-width // LANES) * LANES
    height = depth * NX * 2 * NY * CORES
    scale = 0.2 * math.sqrt(max(height, width))
    half, single = jnp.bfloat16, jnp.float32
    dma = pltpu.SemaphoreType.DMA
    totals, finals = pl.pallas_call(
        kernel,
        out_shape=[
            jax.ShapeDtypeStruct(momentum.shape, single),
            jax.ShapeDtypeStruct((count, depth, wide), half),
        ],
        in_specs=[pl.BlockSpec(memory_space=pltpu.HBM)] * 2,
        out_specs=[pl.BlockSpec(memory_space=pltpu.VMEM)] * 2,
        scratch_shapes=[
            pltpu.VMEM((count, depth, width), single),
            pltpu.VMEM((count, depth, width), single),
            pltpu.VMEM((count, depth, width), single),
            pltpu.VMEM((NZ, CORES, depth, width), single),
            pltpu.VMEM((2 * CORES, depth, width), single),
            pltpu.VMEM((NX, NY, 2 * CORES * depth, wide), half),
            pltpu.VMEM((wide, wide), single),
            pltpu.VMEM((2 * CORES, depth, wide), half),
            dma((2,)),
            dma((PODS,)),
            dma((NZ, CORES)),
            dma((NY - 1,)),
            dma((NY,)),
            dma((NX - 1, NY)),
            dma((NX - 1, NY)),
            dma((NZ, CORES)),
            dma((PODS,)),
            dma((NZ, CORES)),
            dma((PODS,)),
        ],
        compiler_params=pltpu.CompilerParams(
            collective_id=0, has_side_effects=True, vmem_limit_bytes=VMEM_LIMIT
        ),
    )(
        pltpu.with_memory_space_constraint(grads, pltpu.HBM),
        pltpu.with_memory_space_constraint(momentum, pltpu.HBM),
    )
    return pl.pallas_call(
        functools.partial(finish, scale),
        out_shape=[jax.ShapeDtypeStruct(momentum.shape, single)] * 2,
        in_specs=[pl.BlockSpec(memory_space=pltpu.VMEM)] * 3,
        out_specs=[pl.BlockSpec(memory_space=pltpu.HBM)] * 2,
        scratch_shapes=[
            pltpu.VMEM(momentum.shape, single),
            pltpu.VMEM(momentum.shape, single),
            dma((2,)),
        ],
        compiler_params=pltpu.CompilerParams(vmem_limit_bytes=VMEM_LIMIT),
    )(totals, finals, momentum)


def solution(mesh):
    in_specs = (P("outer", None, "dp", None), P(None, "dp", None))
    out_specs = (P(None, "dp", None), P(None, "dp", None))
    return jax.shard_map(
        per_device, mesh=mesh, in_specs=in_specs, out_specs=out_specs, check_vma=False
    )
```
